32 devices in a mesh: tm: 16 (over z, y, x), space: 2 (over core).
Axes of the slice: x: 2, y: 2, z: 4, core: 2. Of those that a mesh axis runs over, the one named last changes fastest.
Arguments:
- window_state: float32 [16, 512, 512], P('tm', 'space'), may hold values from -6 to 6
- prior_window: float32 [16, 512, 512], P('tm', 'space'), may hold values from -6 to 6
- conductivity: float32 [512, 512], P('space'), may hold values from 0.5 to 2
Outputs:
- updated: float32 [16, 512, 512], P('tm', 'space')
The draws below stay inside these ranges and needn't reach their ends.
All inputs are finite; a program needn't handle non-finite values.
Results may differ from the reference program's by a relative error of at most 0.0003.
Values sent between devices are 32-bit elements; how exact they have to be, the bound alone decides.
No kernel may reach another device: no remote copies, remote signals or barrier semaphores. Data moves between devices by JAX's collectives and lax.ppermute only.
A program may use at most 64 MiB of HBM per device.

```python
import math
import jax
import jax.numpy as jnp
from jax import lax

NX = 512
NY = 512
SWEEPS = 24
STEPS = 16


def steps_of(stream_key, extent, shards, least, high):
    loudness = 1.0
    for position, shards_of in shards:
        steps = jax.random.uniform(jax.random.fold_in(jax.random.fold_in(stream_key, 6), position), (shards_of,), jnp.float32, least / len(shards), high / len(shards))
        loudness = loudness * jnp.repeat(jnp.exp(steps), extent[position] // shards_of).reshape((-1,) + (1,) * (len(extent) - 1 - position))
    return loudness


def centred(stream_key, dims, width, reach, split=(), kind=jnp.bfloat16):
    entries = jax.random.normal(stream_key, dims, jnp.float32) * width
    if len(split) > 0:
        entries = steps_of(stream_key, dims, split, -0.22, 0.18) * entries
    return jnp.clip(entries, min=-reach, max=reach).astype(kind)


def setup_inputs(seed: int = 0) -> dict:
    streams_of = jax.random.split(jax.random.key(seed), 4)
    return {
        "window_state": centred(streams_of[0], (STEPS, NX, NY), 1.0, 6.0, ((0, 16), (1, 2)), jnp.float32),
        "prior_window": centred(streams_of[1], (STEPS, NX, NY), 1.0, 6.0, ((0, 16), (1, 2)), jnp.float32),
        "conductivity": jnp.clip(jnp.exp(math.log(2.0) - 1.3862944 * jax.random.uniform(streams_of[2], (NX, NY), jnp.float32) ** steps_of(streams_of[2], (NX, NY), ((0, 2),), -0.2, 0.2)), 0.5, 2.0),
    }


time_ratio = 2.0
window_alpha = 0.01
spectral_bound = 24.0


def conductance(conductivity, values):
    return conductivity * (1.0 + 0.5 * jnp.tanh(values))


def beside_all(padded):
    return (padded[..., :-2, 1:-1], padded[..., 2:, 1:-1], padded[..., 1:-1, :-2], padded[..., 1:-1, 2:])


def flux_of(values_pad, coeff_pad):
    values = values_pad[..., 1:-1, 1:-1]
    coeff = coeff_pad[..., 1:-1, 1:-1]
    summed = jnp.zeros_like(values)
    for near_value, near_coeff in zip(beside_all(values_pad), beside_all(coeff_pad)):
        summed = summed + 0.5 * (coeff + near_coeff) * (near_value - values)
    return summed


def frozen_weights(coeff_pad):
    coeff = coeff_pad[..., 1:-1, 1:-1]
    facing = tuple(0.5 * time_ratio * (coeff + near_coeff) for near_coeff in beside_all(coeff_pad))
    return facing + (facing[0] + facing[1] + facing[2] + facing[3],)


def operator_image(search_pad, shift_value, weights):
    search = search_pad[:, 1:-1, 1:-1]
    nearby_list = beside_all(search_pad)
    nearby = weights[0] * nearby_list[0] + weights[1] * nearby_list[1] + weights[2] * nearby_list[2] + weights[3] * nearby_list[3]
    central = weights[4]
    image_real = shift_value[0] * search[0] - shift_value[1] * search[1] + central * search[0] - nearby[0]
    image_imag = shift_value[0] * search[1] + shift_value[1] * search[0] + central * search[1] - nearby[1]
    return jnp.stack([image_real, image_imag])


def complex_times(left_pair, right_pair):
    return (left_pair[0] * right_pair[0] - left_pair[1] * right_pair[1], left_pair[0] * right_pair[1] + left_pair[1] * right_pair[0])


def complex_inverse(pair_value):
    scaling = 1.0 / (pair_value[0] * pair_value[0] + pair_value[1] * pair_value[1])
    return (pair_value[0] * scaling, -pair_value[1] * scaling)


def scaled_field(pair_value, field_pair):
    return jnp.stack([pair_value[0] * field_pair[0] - pair_value[1] * field_pair[1], pair_value[0] * field_pair[1] + pair_value[1] * field_pair[0]])


def frequency_scalars(frequency, length):
    angle = 2.0 * math.pi * frequency.astype(jnp.float32) / length
    beta = math.exp(math.log(window_alpha) / length)
    shift_value = (1.0 - beta * jnp.cos(angle), beta * jnp.sin(angle))
    half_span = 0.5 * spectral_bound * time_ratio
    center = (shift_value[0] + half_span, shift_value[1])
    relative = (center[0] / half_span, center[1] / half_span)
    return shift_value, center, relative, half_span


def chebyshev(source_pair, center, relative, half_span, apply_op, inside):
    search = scaled_field(complex_inverse(center), source_pair) * inside
    factor = complex_inverse(relative)

    def one_sweep(counter, carried):
        solution, remain, search, factor_real, factor_imag = carried
        applied = apply_op(search)
        solution = solution + search
        remain = remain - applied
        renewed = complex_inverse((2.0 * relative[0] - factor_real, 2.0 * relative[1] - factor_imag))
        lead_factor = complex_times(renewed, (factor_real, factor_imag))
        rest_factor = (2.0 * renewed[0] / half_span, 2.0 * renewed[1] / half_span)
        search = (scaled_field(lead_factor, search) + scaled_field(rest_factor, remain)) * inside
        return solution, remain, search, renewed[0], renewed[1]

    initial = (jnp.zeros_like(source_pair), source_pair, search, factor[0], factor[1])
    solution, remain, search, factor_real, factor_imag = lax.fori_loop(0, SWEEPS, one_sweep, initial)
    return solution + search


def reference(window_state, prior_window, conductivity):
    length = window_state.shape[0]
    initial = prior_window[length - 1]
    before = jnp.concatenate([initial[None], window_state[:-1]], axis=0)
    coeff = conductance(conductivity[None], window_state)
    values_pad = jnp.pad(window_state, ((0, 0), (1, 1), (1, 1)))
    coeff_pad = jnp.pad(coeff, ((0, 0), (1, 1), (1, 1)))
    residual = before - window_state + time_ratio * flux_of(values_pad, coeff_pad)
    counter = jnp.arange(length).astype(jnp.float32)
    damping = jnp.exp(counter * (math.log(window_alpha) / length))
    spectrum = jnp.fft.fft(residual * damping[:, None, None], axis=0)
    spec_real = jnp.real(spectrum)
    spec_imag = jnp.imag(spectrum)
    frozen = conductance(conductivity, initial)
    weights = frozen_weights(jnp.pad(frozen, 1))

    def solve_one(element):
        frequency, part_real, part_imag = element
        shift_value, center, relative, half_span = frequency_scalars(frequency, length)

        def apply_op(search):
            return operator_image(jnp.pad(search, ((0, 0), (1, 1), (1, 1))), shift_value, weights)

        return chebyshev(jnp.stack([part_real, part_imag]), center, relative, half_span, apply_op, 1.0)

    solved = lax.map(solve_one, (jnp.arange(length).astype(jnp.int32), spec_real, spec_imag))
    combined = solved[:, 0] + 1j * solved[:, 1]
    correction = jnp.real(jnp.fft.ifft(combined, axis=0)) / damping[:, None, None]
    return window_state + correction
```

```python
import functools
import math

import jax
import jax.numpy as jnp
import numpy as np
from jax import lax
from jax.experimental import pallas as pl
from jax.experimental.pallas import tpu as pltpu
from jax.sharding import PartitionSpec as P

SWEEPS = 24
MARGIN = SWEEPS + 4
LANES = 128
WIDTH = LANES // 2
EDGE = 32

time_ratio = 2.0
window_alpha = 0.01
spectral_bound = 24.0

VMEM = pl.BlockSpec(memory_space=pltpu.VMEM)
VMEM_LIMIT = 60 * 1024 * 1024


def sweep_table(length):
    beta = math.exp(math.log(window_alpha) / length)
    half = 0.5 * spectral_bound * time_ratio

    def times_y(p):
        out = np.zeros_like(p)
        out[1:] += 0.5 * p[:-1]
        out[:-1] += 0.5 * p[1:]
        out[1] += 0.5 * p[0]
        return out

    def series(j):
        angle = 2.0 * math.pi * j / length
        shift = complex(1.0 - beta * math.cos(angle), beta * math.sin(angle))
        if j == 0 or 2 * j == length:
            shift = complex(shift.real, 0.0)
        center = shift + half
        rel = center / half
        x = np.zeros(SWEEPS + 3, np.complex128)
        r = x.copy()
        r[0] = 1.0
        d = r / center
        rho = 1.0 / rel
        for _ in range(SWEEPS):
            image = center * d - half * times_y(d)
            x = x + d
            r = r - image
            rho2 = 1.0 / (2.0 * rel - rho)
            d = rho2 * rho * d + (2.0 * rho2 / half) * r
            rho = rho2
        x = x + d
        second = 0.5 * x
        second[0] = x[0]
        second[:-2] -= 0.5 * x[2:]
        return second[: SWEEPS + 1]

    pairs = length // 2
    table = np.zeros((pairs, SWEEPS + 1, 4))
    for p in range(pairs):
        g = series(p)
        if p == 0:
            last = series(pairs)
            table[p] = np.stack([g.real, 0 * g.real, 0 * g.real, last.real], axis=1)
        else:
            table[p] = np.stack([g.real, -g.imag, g.imag, g.real], axis=1)
    return table.reshape(pairs // 8, 8, SWEEPS + 1, 4).transpose(0, 2, 3, 1).astype(np.float32)


def turned(value, angle):
    re, im = value
    c, s = math.cos(angle), math.sin(angle)
    if abs(s) < 1e-12:
        return (re * c if c != 1.0 else re), (None if im is None else im * c if c != 1.0 else im)
    if abs(c) < 1e-12:
        return (None if im is None else -im * s if s != -1.0 else im), (re * s if s != -1.0 else -re)
    if im is None:
        return re * c, re * s
    return re * c - im * s, re * s + im * c


def plus(a, b):
    return b if a is None else a if b is None else a + b


def minus(a, b):
    return a if b is None else -b if a is None else a - b


def negative(a):
    return None if a is None else -a


def real_dft(fields):
    count = len(fields)
    if count == 1:
        return [(fields[0], None)]
    even, odd = real_dft(fields[0::2]), real_dft(fields[1::2])
    out = [None] * (count // 2 + 1)
    for j in range(count // 4 + 1):
        if count == 2:
            e, o = even[0], odd[0]
        else:
            e, o = even[j], odd[j]
        t = turned(o, -2.0 * math.pi * j / count)
        mirror = (minus(e[0], t[0]), negative(minus(e[1], t[1])))
        out[count // 2 - j] = mirror
        out[j] = (plus(e[0], t[0]), plus(e[1], t[1]))
    out[0] = (out[0][0], None)
    out[-1] = (out[-1][0], None)
    return out


def real_inverse(spectrum):
    count = 2 * (len(spectrum) - 1)
    if count == 2:
        a, b = spectrum[0][0], spectrum[1][0]
        return [a + b, a - b]
    even, odd = [], []
    for j in range(count // 4 + 1):
        a, b = spectrum[j], spectrum[count // 2 - j]
        even.append((plus(a[0], b[0]), minus(a[1], b[1])))
        t = (minus(a[0], b[0]), plus(a[1], b[1]))
        odd.append(turned_full(t, 2.0 * math.pi * j / count))
    even[0] = (even[0][0], None)
    even[-1] = (even[-1][0], None)
    odd[0] = (odd[0][0], None)
    odd[-1] = (odd[-1][0], None)
    even, odd = real_inverse(even), real_inverse(odd)
    return [v for pair in zip(even, odd) for v in pair]


def turned_full(value, angle):
    re, im = value
    if re is None:
        c, s = math.cos(angle), math.sin(angle)
        return (-im * s if abs(s) > 1e-12 else None), (im * c if abs(c) > 1e-12 else None)
    return turned(value, angle)


def conductance(conductivity, values):
    return conductivity * (1.0 + 0.5 * jnp.tanh(values))


def roll(x, amount):
    return pltpu.roll(x, amount % LANES, x.ndim - 1)


def lane_index():
    return lax.broadcasted_iota(jnp.int32, (8, LANES), 1)


def pack_kernel(rows, w_ref, prior_ref, cond_ref, edge_ref, place_ref, w_out, prior_out, cond_out, ext):
    height, columns = w_ref.shape
    tiles = columns // LANES
    lane = lane_index()
    deep = w_out.shape[1]
    across = columns // WIDTH
    first = place_ref[0] == 0
    last = place_ref[1] == 1

    def fill(which, ref):
        for c in range(tiles):
            cols = pl.ds(c * LANES, LANES)
            edge = edge_ref[which, :, cols]
            ext[c, pl.ds(0, EDGE), :] = jnp.where(first, 0.0, edge)
            ext[c, pl.ds(EDGE + height, EDGE), :] = jnp.where(last, 0.0, edge)
            for t in range(0, height, 64):
                ext[c, pl.ds(EDGE + t, 64), :] = ref[pl.ds(t, 64), cols]

    def tile_at(start, c):
        if c < 0 or c >= tiles:
            return jnp.zeros((8, LANES), jnp.float32)
        return ext[c, pl.ds(start, 8), :]

    def block_tile(start, cb):
        if cb % 2 == 0:
            a, b = tile_at(start, cb // 2 - 1), tile_at(start, cb // 2)
            return roll(jnp.where(lane < LANES - EDGE, b, a), EDGE)
        a, b = tile_at(start, cb // 2), tile_at(start, cb // 2 + 1)
        return roll(jnp.where(lane < EDGE, b, a), -EDGE)

    def spread(out):
        for rb in range(height // rows):
            def step(t, _):
                start = rb * rows + EDGE - MARGIN + t * 8
                for cb in range(across):
                    out[rb * across + cb, pl.ds(pl.multiple_of(t * 8, 8), 8), :] = block_tile(start, cb)
                return 0
            lax.fori_loop(0, deep // 8, step, 0)

    fill(1, prior_ref)
    spread(prior_out)
    fill(0, w_ref)
    spread(w_out)
    fill(2, cond_ref)
    rb, cb = place_ref[2], place_ref[3]
    for c in range(across):
        @pl.when(cb == c)
        def _():
            def step(t, _):
                cond_out[pl.ds(pl.multiple_of(t * 8, 8), 8), :] = block_tile(rb * rows + EDGE - MARGIN + t * 8, c)
                return 0
            lax.fori_loop(0, deep // 8, step, 0)


def solve_kernel(
    length, rows, limits, w_ref, prior_ref, cond_ref, table_ref, place_ref, out_ref,
    coeff, field, other, total, frozen, south, east, west, middle,
):
    deep = w_ref.shape[1]
    pairs = length // 2
    groups = pairs // 8
    low = MARGIN - SWEEPS
    lane = lane_index()
    sub = lax.broadcasted_iota(jnp.int32, (8, LANES), 0)
    row0, col0 = place_ref[4], place_ref[5]
    inside_lane = (lane + col0 >= 0) & (lane + col0 < limits[1])
    beta = math.exp(math.log(window_alpha) / length)
    half = 0.5 * spectral_bound * time_ratio
    scale = 0.5 * time_ratio * 2.0 / half

    def coefficients(t, _):
        at = pl.ds(pl.multiple_of(t * 8, 8), 8)
        cond = cond_ref[at, :]
        frozen[at, :] = conductance(cond, prior_ref[at, :])
        for n in range(length):
            coeff[n, at, :] = conductance(cond, w_ref[n, at, :])
        return 0

    lax.fori_loop(0, deep // 8, coefficients, 0)

    def residuals(t, _):
        start = low + t * 8
        here, above, below = pl.ds(start, 8), pl.ds(start - 1, 8), pl.ds(start + 1, 8)
        row = sub + (row0 + start)
        inside = inside_lane & (row >= 0) & (row < limits[0])
        q, qn, qs = frozen[here, :], frozen[above, :], frozen[below, :]
        qe, qw = roll(q, -1), roll(q, 1)
        middle[here, :] = 2.0 - scale * (4.0 * q + qn + qs + qe + qw)
        south[here, :] = jnp.where(inside & (row + 1 < limits[0]), scale * (q + qs), 0.0)
        ew = jnp.where(inside & (lane + col0 + 1 < limits[1]), scale * (q + qe), 0.0)
        east[here, :] = ew
        west[here, :] = roll(ew, 1)
        fields = []
        for n in range(length):
            v, vn, vs = w_ref[n, here, :], w_ref[n, above, :], w_ref[n, below, :]
            c, cn, cs = coeff[n, here, :], coeff[n, above, :], coeff[n, below, :]
            fe = (c + roll(c, -1)) * (roll(v, -1) - v)
            fs = (c + cs) * (vs - v)
            fn = (c + cn) * (vn - v)
            flux = (0.5 * time_ratio) * (fe - roll(fe, 1) + fs + fn)
            before = prior_ref[here, :] if n == 0 else w_ref[n - 1, here, :]
            r = jnp.where(inside, before - v + flux, 0.0)
            fields.append(r * (beta**n))
        spectrum = real_dft(fields)
        for p in range(pairs):
            re = spectrum[p][0]
            im = spectrum[pairs][0] if p == 0 else spectrum[p][1]
            base = (p // 8) * deep * 16 + start * 16 + p % 8
            field[pl.ds(base, 8, stride=16), :] = re
            field[pl.ds(base + 8, 8, stride=16), :] = im
        return 0

    south[pl.ds(0, 8), :] = jnp.zeros((8, LANES), jnp.float32)
    lax.fori_loop(0, (rows + 2 * SWEEPS) // 8, residuals, 0)

    unroll = 4

    def sweeps(g, _):
        offset = g * (deep * 16)
        xoffset = g * (rows * 16)

        def one(level, cur, new, first):
            halo = -(-(SWEEPS - level) // unroll) * unroll
            adds = level % 2 == 1 or level == SWEEPS
            if adds:
                h = [table_ref[g, level, i] for i in range(4)]
                if level % 2 == 1:
                    hp = [table_ref[g, level - 1, i] for i in range(4)]

            def load(i):
                at = pl.multiple_of(offset + i * 16, 16)
                return cur[pl.ds(at, 8), :], cur[pl.ds(at + 8, 8), :]

            def weight(ref, i):
                return ref[pl.ds(i, 8, stride=0), :]

            def segment(start, count, add, carry):
                def step(u, carry):
                    an, bn, ac, bc, wn = carry
                    for v in range(unroll):
                        i = start + u * unroll + v
                        a_s, b_s = load(i + 1)
                        ws, we, ww, wc = (weight(r, i) for r in (south, east, west, middle))
                        at = pl.multiple_of(offset + i * 16, 16)
                        ka, kb = pl.ds(at, 8), pl.ds(at + 8, 8)
                        na = wc * ac + wn * an + ws * a_s + we * roll(ac, -1) + ww * roll(ac, 1)
                        nb = wc * bc + wn * bn + ws * b_s + we * roll(bc, -1) + ww * roll(bc, 1)
                        if not first:
                            na = na - new[ka, :]
                            nb = nb - new[kb, :]
                        if level < SWEEPS:
                            new[ka, :] = na
                            new[kb, :] = nb
                        if add:
                            xt = pl.multiple_of(xoffset + (i - MARGIN) * 16, 16)
                            xa, xb = pl.ds(xt, 8), pl.ds(xt + 8, 8)
                            pa = h[0] * na + h[1] * nb
                            pb = h[2] * na + h[3] * nb
                            if level % 2 == 1:
                                pa = pa + (hp[0] * ac + hp[1] * bc)
                                pb = pb + (hp[2] * ac + hp[3] * bc)
                            if not first:
                                pa = pa + total[xa, :]
                                pb = pb + total[xb, :]
                            total[xa, :] = pa
                            total[xb, :] = pb
                        an, bn, ac, bc, wn = ac, bc, a_s, b_s, ws
                    return an, bn, ac, bc, wn

                return lax.fori_loop(0, count // unroll, step, carry)

            begin = MARGIN - halo
            carry = load(begin - 1) + load(begin) + (weight(south, begin - 1),)
            if halo:
                carry = segment(begin, halo, False, carry)
            carry = segment(MARGIN, rows, adds, carry)
            if halo:
                segment(MARGIN + rows, halo, False, carry)

        one(1, field, other, True)
        for level in range(2, SWEEPS + 1):
            if level % 2 == 0:
                one(level, other, field, False)
            else:
                one(level, field, other, False)
        return 0

    if groups == 1:
        sweeps(0, 0)
    else:
        lax.fori_loop(0, groups, sweeps, 0)

    keep = rows // 2

    def inverse(start):
        spectrum = []
        nyquist = None
        for p in range(pairs):
            base = (p // 8) * rows * 16 + start * 16 + p % 8
            re = total[pl.ds(base, 8, stride=16), :]
            im = total[pl.ds(base + 8, 8, stride=16), :]
            if p == 0:
                nyquist = im
                im = None
            spectrum.append((re, im))
        spectrum.append((nyquist, None))
        return real_inverse(spectrum)

    def finish(t, _):
        lower, upper = inverse(t * 8), inverse(keep + t * 8)
        for n in range(length):
            factor = beta ** (-n) / length
            merged = jnp.where(lane < WIDTH, roll(lower[n], -EDGE), roll(upper[n], EDGE))
            out_ref[n, pl.ds(pl.multiple_of(t * 8, 8), 8), :] = merged * factor
        return 0

    lax.fori_loop(0, keep // 8, finish, 0)


def merge_kernel(rows, w_ref, got_ref, out_ref):
    height, columns = w_ref.shape
    across = columns // WIDTH
    keep = rows // 2
    lane = lane_index()
    for rb in range(height // rows):
        def step(t, _):
            at = pl.ds(pl.multiple_of(t * 8, 8), 8)
            for pair in range(across // 2):
                a = got_ref[rb * across + 2 * pair, at, :]
                b = got_ref[rb * across + 2 * pair + 1, at, :]
                upper = jnp.where(lane < WIDTH, a, roll(b, WIDTH))
                lower = jnp.where(lane < WIDTH, roll(a, WIDTH), b)
                cols = pl.ds(pair * LANES, LANES)
                one = pl.ds(pl.multiple_of(rb * rows + t * 8, 8), 8)
                two = pl.ds(pl.multiple_of(rb * rows + keep + t * 8, 8), 8)
                out_ref[one, cols] = w_ref[one, cols] + upper
                out_ref[two, cols] = w_ref[two, cols] + lower
            return 0
        lax.fori_loop(0, keep // 8, step, 0)


def scattered(blocks, axis):
    count = lax.axis_size(axis)
    index = lax.axis_index(axis)
    owner = count - 1
    stride = 1
    current = blocks
    while stride < count:
        radix = 4 if (count // stride) % 4 == 0 else count // stride
        rest = count // (stride * radix)
        current = current.reshape((rest, radix) + current.shape[1:])
        base = [owner - (stride - 1) + low for low in range(stride)]
        digit = (index // stride) % radix
        kept = jnp.where(digit == radix - 1, current[:, radix - 1], 0.0)
        for value in range(radix - 1):
            route = [(b, b - stride * (radix - 1 - value)) for b in base]
            kept = kept + lax.ppermute(current[:, value], axis, route)
        current = kept
        stride *= radix
    return current[0]


def body(window_state, prior_window, conductivity):
    length = lax.axis_size("tm")
    halves = lax.axis_size("space")
    height, columns = window_state.shape[1:]
    across = columns // WIDTH
    rows = height * across // length
    deep = rows + 2 * MARGIN
    step_index = lax.axis_index("tm")
    half_index = lax.axis_index("space")
    state = window_state[0]

    lowest = half_index == 0
    edges = jnp.stack(
        [jnp.where(lowest, x[-EDGE:], x[:EDGE]) for x in (state, prior_window[0], conductivity)]
    )
    edges = lax.ppermute(edges, "space", [(0, 1), (1, 0)])
    rb, cb = step_index // across, step_index % across
    place = jnp.stack(
        [
            half_index,
            (half_index == halves - 1).astype(jnp.int32),
            rb,
            cb,
            half_index * height + rb * rows - MARGIN,
            cb * WIDTH - EDGE,
        ]
    ).astype(jnp.int32)

    shape = jax.ShapeDtypeStruct
    params = pltpu.CompilerParams(vmem_limit_bytes=VMEM_LIMIT)
    smem = pl.BlockSpec(memory_space=pltpu.SMEM)
    sent, prior_blocks, cond = pl.pallas_call(
        functools.partial(pack_kernel, rows),
        name="pack",
        out_shape=[
            shape((length, deep, LANES), jnp.float32),
            shape((length, deep, LANES), jnp.float32),
            shape((deep, LANES), jnp.float32),
        ],
        in_specs=[VMEM] * 4 + [smem],
        out_specs=[VMEM] * 3,
        scratch_shapes=[pltpu.VMEM((columns // LANES, height + 2 * EDGE, LANES), jnp.float32)],
        compiler_params=params,
    )(state, prior_window[0], conductivity, edges, place)

    got = lax.all_to_all(sent, "tm", split_axis=0, concat_axis=0, tiled=True)
    prior = scattered(prior_blocks, "tm")

    table = sweep_table(length)
    table = jnp.broadcast_to(jnp.asarray(table)[..., None], table.shape + (LANES,))
    flat = pltpu.VMEM((length * deep, LANES), jnp.float32)
    plane = pltpu.VMEM((deep, LANES), jnp.float32)
    correction = pl.pallas_call(
        functools.partial(solve_kernel, length, rows, (height * halves, columns)),
        name="solve",
        out_shape=shape((length, rows // 2, LANES), jnp.float32),
        in_specs=[VMEM] * 4 + [smem],
        out_specs=VMEM,
        scratch_shapes=[
            pltpu.VMEM((length, deep, LANES), jnp.float32),
            flat,
            flat,
            pltpu.VMEM((length * rows, LANES), jnp.float32),
            plane,
            plane,
            plane,
            plane,
            plane,
        ],
        compiler_params=params,
    )(got, prior, cond, table, place)

    back = lax.all_to_all(correction, "tm", split_axis=0, concat_axis=0, tiled=True)
    updated = pl.pallas_call(
        functools.partial(merge_kernel, rows),
        name="merge",
        out_shape=shape((height, columns), jnp.float32),
        in_specs=[VMEM] * 2,
        out_specs=VMEM,
        compiler_params=params,
    )(state, back)
    return updated[None]


def solution(mesh):
    in_specs = (P("tm", "space", None), P("tm", "space", None), P("space", None))
    out_specs = P("tm", "space", None)
    return jax.shard_map(body, mesh=mesh, in_specs=in_specs, out_specs=out_specs, check_vma=False)
```

```python
import functools
import math

import jax
import jax.numpy as jnp
import numpy as np
from jax import lax
from jax.experimental import pallas as pl
from jax.experimental.pallas import tpu as pltpu
from jax.sharding import PartitionSpec as P

SWEEPS = 24
LANES = 128
WIDTH = LANES // 2
EDGE = 32
AHEAD = 6

time_ratio = 2.0
window_alpha = 0.01
spectral_bound = 24.0

HALO_AHEAD = 6
CENTER_STEP = 16
VMEM = pl.BlockSpec(memory_space=pltpu.VMEM)
VMEM_LIMIT = 20 * 1024 * 1024
SMEM = pl.BlockSpec(memory_space=pltpu.SMEM)


def sweep_table(length):
    beta = math.exp(math.log(window_alpha) / length)
    half = 0.5 * spectral_bound * time_ratio

    def times_y(p):
        out = np.zeros_like(p)
        out[1:] += 0.5 * p[:-1]
        out[:-1] += 0.5 * p[1:]
        out[1] += 0.5 * p[0]
        return out

    def series(j):
        angle = 2.0 * math.pi * j / length
        shift = complex(1.0 - beta * math.cos(angle), beta * math.sin(angle))
        if j == 0 or 2 * j == length:
            shift = complex(shift.real, 0.0)
        center = shift + half
        rel = center / half
        x = np.zeros(SWEEPS + 3, np.complex128)
        r = x.copy()
        r[0] = 1.0
        d = r / center
        rho = 1.0 / rel
        for _ in range(SWEEPS):
            image = center * d - half * times_y(d)
            x = x + d
            r = r - image
            rho2 = 1.0 / (2.0 * rel - rho)
            d = rho2 * rho * d + (2.0 * rho2 / half) * r
            rho = rho2
        x = x + d
        second = 0.5 * x
        second[0] = x[0]
        second[:-2] -= 0.5 * x[2:]
        return second[: SWEEPS + 1]

    pairs = length // 2
    table = np.zeros((pairs, SWEEPS + 1, 4))
    for p in range(pairs):
        g = series(p)
        if p == 0:
            last = series(pairs)
            table[p] = np.stack([g.real, 0 * g.real, 0 * g.real, last.real], axis=1)
        else:
            table[p] = np.stack([g.real, -g.imag, g.imag, g.real], axis=1)
    return table.reshape(pairs // 8, 8, SWEEPS + 1, 4).transpose(0, 2, 3, 1).astype(np.float32)


def turned(value, angle):
    re, im = value
    c, s = math.cos(angle), math.sin(angle)
    if abs(s) < 1e-12:
        return (re * c if c != 1.0 else re), (None if im is None else im * c if c != 1.0 else im)
    if abs(c) < 1e-12:
        return (None if im is None else -im * s if s != -1.0 else im), (re * s if s != -1.0 else -re)
    if im is None:
        return re * c, re * s
    return re * c - im * s, re * s + im * c


def plus(a, b):
    return b if a is None else a if b is None else a + b


def minus(a, b):
    return a if b is None else -b if a is None else a - b


def negative(a):
    return None if a is None else -a


def real_dft(fields):
    count = len(fields)
    if count == 1:
        return [(fields[0], None)]
    even, odd = real_dft(fields[0::2]), real_dft(fields[1::2])
    out = [None] * (count // 2 + 1)
    for j in range(count // 4 + 1):
        if count == 2:
            e, o = even[0], odd[0]
        else:
            e, o = even[j], odd[j]
        t = turned(o, -2.0 * math.pi * j / count)
        mirror = (minus(e[0], t[0]), negative(minus(e[1], t[1])))
        out[count // 2 - j] = mirror
        out[j] = (plus(e[0], t[0]), plus(e[1], t[1]))
    out[0] = (out[0][0], None)
    out[-1] = (out[-1][0], None)
    return out


def real_inverse(spectrum):
    count = 2 * (len(spectrum) - 1)
    if count == 2:
        a, b = spectrum[0][0], spectrum[1][0]
        return [a + b, a - b]
    even, odd = [], []
    for j in range(count // 4 + 1):
        a, b = spectrum[j], spectrum[count // 2 - j]
        even.append((plus(a[0], b[0]), minus(a[1], b[1])))
        t = (minus(a[0], b[0]), plus(a[1], b[1]))
        odd.append(turned_full(t, 2.0 * math.pi * j / count))
    even[0] = (even[0][0], None)
    even[-1] = (even[-1][0], None)
    odd[0] = (odd[0][0], None)
    odd[-1] = (odd[-1][0], None)
    even, odd = real_inverse(even), real_inverse(odd)
    return [v for pair in zip(even, odd) for v in pair]


def turned_full(value, angle):
    re, im = value
    if re is None:
        c, s = math.cos(angle), math.sin(angle)
        return (-im * s if abs(s) > 1e-12 else None), (im * c if abs(c) > 1e-12 else None)
    return turned(value, angle)


def conductance(conductivity, values):
    return conductivity * (1.0 + 0.5 * jnp.tanh(values))


def roll(x, amount):
    return pltpu.roll(x, amount % LANES, x.ndim - 1)


def lane_index():
    return lax.broadcasted_iota(jnp.int32, (8, LANES), 1)


def patch(tiles, lane, cb):
    zero = jnp.zeros((8, LANES), jnp.float32)
    tile = lambda c: tiles[c] if 0 <= c < len(tiles) else zero
    if cb % 2 == 0:
        return roll(jnp.where(lane < LANES - EDGE, tile(cb // 2), tile(cb // 2 - 1)), EDGE)
    return roll(jnp.where(lane < EDGE, tile(cb // 2 + 1), tile(cb // 2)), -EDGE)


def pack_kernel(place_ref, field_ref, out_ref):
    bands, height, columns = field_ref.shape
    flip = place_ref[0]
    lane = lane_index()
    for t in range(height // 8):
        at = pl.ds(t * 8, 8)
        for band in range(bands):
            tiles = [field_ref[band, at, pl.ds(c * LANES, LANES)] for c in range(columns // LANES)]
            for cb in range(columns // WIDTH):
                out_ref[cb, lax.bitwise_xor(band, flip), at, :] = patch(tiles, lane, cb)


def own_kernel(place_ref, field_ref, out_ref):
    height, columns = field_ref.shape[1:]
    band, block = place_ref[1], place_ref[2]
    lane = lane_index()
    for cb in range(columns // WIDTH):
        @pl.when(block == cb)
        def _():
            for t in range(height // 8):
                at = pl.ds(t * 8, 8)
                tiles = [field_ref[band, at, pl.ds(c * LANES, LANES)] for c in range(columns // LANES)]
                out_ref[at, :] = patch(tiles, lane, cb)


def solve_kernel(
    length, limits, place_ref, w_ref, wa_ref, wb_ref, own_ref, owna_ref, ownb_ref, table_ref, out_ref,
    state, coeff, field, other, total, prior, frozen, south, east, west, middle,
):
    rows = w_ref.shape[1]
    deep = state.shape[1]
    pairs = length // 2
    groups = pairs // 8
    low = EDGE - SWEEPS
    lane = lane_index()
    sub = lax.broadcasted_iota(jnp.int32, (8, LANES), 0)
    row0, col0 = place_ref[3], place_ref[4]
    inside_lane = (lane + col0 >= 0) & (lane + col0 < limits[1])
    beta = math.exp(math.log(window_alpha) / length)
    half = 0.5 * spectral_bound * time_ratio
    scale = 0.5 * time_ratio * 2.0 / half

    def edge_pair(first, second):
        def read(a, b, n, at):
            return jnp.where(first == 1, a[n, at, :], jnp.where(second == 1, b[n, at, :], 0.0))
        return read

    def gather(base, count, read, center):
        def step(t, _):
            at = pl.ds(pl.multiple_of(t * 8, 8), 8)
            to = pl.ds(pl.multiple_of(base + t * 8, 8), 8)
            p, cond = (own_ref[i, at, :] if center else read(owna_ref, ownb_ref, i, at) for i in range(2))
            prior[to, :] = p
            frozen[to, :] = conductance(cond, p)
            for n in range(length):
                v = w_ref[n, at, :] if center else read(wa_ref, wb_ref, n, at)
                state[n, to, :] = v
                coeff[n, to, :] = conductance(cond, v)
            return 0

        lax.fori_loop(0, count // 8, step, 0)

    gather(0, EDGE, edge_pair(place_ref[5], place_ref[6]), False)
    gather(EDGE, rows, None, True)
    gather(EDGE + rows, EDGE, edge_pair(place_ref[7], place_ref[8]), False)

    def residuals(t, _):
        start = low + t * 8
        here, above, below = pl.ds(start, 8), pl.ds(start - 1, 8), pl.ds(start + 1, 8)
        row = sub + (row0 + start)
        inside = inside_lane & (row >= 0) & (row < limits[0])
        q, qn, qs = frozen[here, :], frozen[above, :], frozen[below, :]
        qe, qw = roll(q, -1), roll(q, 1)
        middle[here, :] = 2.0 - scale * (4.0 * q + qn + qs + qe + qw)
        south[here, :] = jnp.where(inside & (row + 1 < limits[0]), scale * (q + qs), 0.0)
        ew = jnp.where(inside & (lane + col0 + 1 < limits[1]), scale * (q + qe), 0.0)
        east[here, :] = ew
        west[here, :] = roll(ew, 1)
        fields = []
        for n in range(length):
            v, vn, vs = state[n, here, :], state[n, above, :], state[n, below, :]
            c, cn, cs = coeff[n, here, :], coeff[n, above, :], coeff[n, below, :]
            fe = (c + roll(c, -1)) * (roll(v, -1) - v)
            fs = (c + cs) * (vs - v)
            fn = (c + cn) * (vn - v)
            flux = (0.5 * time_ratio) * (fe - roll(fe, 1) + fs + fn)
            before = prior[here, :] if n == 0 else state[n - 1, here, :]
            r = jnp.where(inside, before - v + flux, 0.0)
            fields.append(r * (beta**n))
        spectrum = real_dft(fields)
        for p in range(pairs):
            re = spectrum[p][0]
            im = spectrum[pairs][0] if p == 0 else spectrum[p][1]
            base = (p // 8) * deep * 16 + start * 16 + p % 8
            field[pl.ds(base, 8, stride=16), :] = re
            field[pl.ds(base + 8, 8, stride=16), :] = im
        return 0

    south[pl.ds(0, 8), :] = jnp.zeros((8, LANES), jnp.float32)
    lax.fori_loop(0, (rows + 2 * SWEEPS) // 8, residuals, 0)

    def sweeps(g, _):
        offset = g * (deep * 16)
        xoffset = g * (rows * 16)

        def rows_at(ref, base, i):
            at = base + i * 16
            return ref[pl.ds(at, 8), :], ref[pl.ds(at + 8, 8), :]

        def weight(ref, i):
            return ref[pl.ds(i, 8, stride=0), :]

        def one(level, cur, new, first):
            begin, end = low + level, deep - low - level

            def across(i, here):
                we, ww = weight(east, i), weight(west, i)
                return tuple(we * roll(x, -1) + ww * roll(x, 1) for x in here)

            load = lambda i: rows_at(cur, offset, i)
            values = {i: load(i) for i in range(begin - 1, begin + AHEAD)}
            flows = {i: across(i, values[i]) for i in range(begin, begin + AHEAD)}
            wn = weight(south, begin - 1)
            for i in range(begin, end):
                j = i + AHEAD
                if j <= end:
                    values[j] = load(j)
                if j < end:
                    flows[j] = across(j, values[j])
                ws, wc = weight(south, i), weight(middle, i)
                flow = flows.pop(i)
                above, here, below = values.pop(i - 1), values[i], values[i + 1]
                for x in range(2):
                    at = pl.ds(offset + i * 16 + 8 * x, 8)
                    value = wc * here[x] + wn * above[x] + ws * below[x]
                    value = value + flow[x]
                    if not first:
                        value = value - new[at, :]
                    new[at, :] = value
                wn = ws

        def accumulate(levels, refs, first):
            terms = [[table_ref[g, level, i] for i in range(4)] for level in levels]
            for i in range(rows):
                parts = [None, None] if first else list(rows_at(total, xoffset, i))
                for h, ref in zip(terms, refs):
                    a, b = rows_at(ref, offset, i + EDGE)
                    for x in range(2):
                        parts[x] = plus(parts[x], h[2 * x] * a + h[2 * x + 1] * b)
                for x in range(2):
                    total[pl.ds(xoffset + i * 16 + 8 * x, 8), :] = parts[x]

        buffers = (field, other)
        for level in range(1, SWEEPS + 1):
            one(level, buffers[(level - 1) % 2], buffers[level % 2], level == 1)
            if level % 2 == 1:
                accumulate((level - 1, level), buffers, level == 1)
        if SWEEPS % 2 == 0:
            accumulate((SWEEPS,), buffers[:1], False)
        return 0

    if groups == 1:
        sweeps(0, 0)
    else:
        lax.fori_loop(0, groups, sweeps, 0)

    keep = rows // 2

    def inverse(start):
        spectrum = []
        nyquist = None
        for p in range(pairs):
            base = (p // 8) * rows * 16 + start * 16 + p % 8
            re = total[pl.ds(base, 8, stride=16), :]
            im = total[pl.ds(base + 8, 8, stride=16), :]
            if p == 0:
                nyquist = im
                im = None
            spectrum.append((re, im))
        spectrum.append((nyquist, None))
        return real_inverse(spectrum)

    def finish(t, _):
        lower, upper = inverse(t * 8), inverse(keep + t * 8)
        for n in range(length):
            factor = beta ** (-n) / length
            merged = jnp.where(lane < WIDTH, roll(lower[n], -EDGE), roll(upper[n], EDGE))
            out_ref[n, pl.ds(pl.multiple_of(t * 8, 8), 8), :] = merged * factor
        return 0

    lax.fori_loop(0, keep // 8, finish, 0)


def merge_kernel(place_ref, w_ref, got_ref, out_ref):
    bands, _, height, columns = w_ref.shape
    flip = place_ref[0]
    lane = lane_index()
    for t in range(height // 8):
        at = pl.ds(t * 8, 8)
        for band in range(bands):
            for pair in range(columns // LANES):
                a = got_ref[2 * pair, lax.bitwise_xor(band, flip), at, :]
                b = got_ref[2 * pair + 1, lax.bitwise_xor(band, flip), at, :]
                cols = pl.ds(pair * LANES, LANES)
                out_ref[band, 0, at, cols] = w_ref[band, 0, at, cols] + jnp.where(lane < WIDTH, a, roll(b, WIDTH))
                out_ref[band, 1, at, cols] = w_ref[band, 1, at, cols] + jnp.where(lane < WIDTH, roll(a, WIDTH), b)


def scattered(blocks, axis):
    count = lax.axis_size(axis)
    index = lax.axis_index(axis)
    owner = count - 1
    stride = 1
    current = blocks
    while True:
        radix = current.shape[0]
        base = [owner - (stride - 1) + low for low in range(stride)]
        digit = (index // stride) % radix
        kept = current[radix - 1]
        for value in range(radix - 1):
            route = [(b, b - stride * (radix - 1 - value)) for b in base]
            kept = jnp.where(digit == value, lax.ppermute(current[value], axis, route), kept)
        stride *= radix
        if stride == count:
            return kept[0]
        current = by_digit(kept, count // stride)


def first_radix(count):
    return 4 if count % 4 == 0 else 2


def by_digit(blocks, count):
    radix = first_radix(count)
    return blocks.reshape((count // radix, radix) + blocks.shape[1:]).swapaxes(0, 1)


def swapped(values, axis, distance=1):
    count = lax.axis_size(axis)
    return lax.ppermute(values, axis, [(i, i ^ distance) for i in range(count)])


def edged_blocks(field, rows):
    halves = lax.axis_size("space")
    up = lax.ppermute(field[:EDGE], "space", [(i + 1, i) for i in range(halves - 1)])
    down = lax.ppermute(field[-EDGE:], "space", [(i, i + 1) for i in range(halves - 1)])
    field = jnp.pad(jnp.concatenate([down, field, up]), ((0, 0), (EDGE, EDGE)))
    height, columns = field.shape
    return jnp.stack(
        [
            field[r : r + rows + 2 * EDGE, c : c + LANES]
            for c in range(0, columns - 2 * EDGE, WIDTH)
            for r in range(0, height - 2 * EDGE, rows)
        ]
    )


def body(window_state, prior_window, conductivity):
    length = lax.axis_size("tm")
    halves = lax.axis_size("space")
    height, columns = window_state.shape[1:]
    across = columns // WIDTH
    rows = height * across // length
    bands = height // rows
    step_index = lax.axis_index("tm")
    half_index = lax.axis_index("space")
    state = window_state[0]
    by_swaps = halves == 2 and bands == 2 and rows >= EDGE
    flip = half_index if by_swaps else 0
    band, block = (step_index % bands) ^ flip, step_index // bands
    overall = half_index * bands + band
    odd = overall % 2
    if by_swaps:
        sides = [odd, (overall == 2), 1 - odd, (overall == 1)]
    else:
        sides = [1, 0, 0, 1]
    place = jnp.stack(
        [
            jnp.asarray(v, jnp.int32)
            for v in [flip, band, block, overall * rows - EDGE, block * WIDTH - EDGE] + sides
        ]
    )

    shape = lambda *dims: jax.ShapeDtypeStruct(dims, jnp.float32)
    params = pltpu.CompilerParams(vmem_limit_bytes=VMEM_LIMIT)

    def packed(field, chunk):
        return pl.pallas_call(
            pack_kernel,
            name="pack",
            grid=(rows // chunk,),
            out_shape=shape(across, bands, rows, LANES),
            in_specs=[SMEM, pl.BlockSpec((bands, chunk, columns), lambda i: (0, i, 0))],
            out_specs=pl.BlockSpec((across, bands, chunk, LANES), lambda i: (0, 0, i, 0)),
            compiler_params=params,
        )(place, field.reshape(bands, rows, columns)).reshape(length, rows, LANES)

    if by_swaps:
        sent = packed(state, 32)
        got = lax.all_to_all(sent, "tm", split_axis=0, concat_axis=0, tiled=True)
        prior = scattered(by_digit(packed(prior_window[0], rows), length), "tm")
        cond = pl.pallas_call(
            own_kernel,
            name="own",
            out_shape=shape(rows, LANES),
            in_specs=[SMEM, VMEM],
            out_specs=VMEM,
            compiler_params=params,
        )(place, conductivity.reshape(bands, rows, columns))
        own = jnp.stack([prior, cond])

        def edges(blocks):
            beside = swapped(jnp.where(odd == 1, blocks[:, :EDGE], blocks[:, -EDGE:]), "tm")
            across_half = swapped(jnp.where(half_index == 1, blocks[:, :EDGE], blocks[:, -EDGE:]), "space")
            return beside, across_half

        parts = (got,) + edges(got) + (own,) + edges(own)
    else:
        got = lax.all_to_all(edged_blocks(state, rows), "tm", split_axis=0, concat_axis=0, tiled=True)
        prior = scattered(by_digit(edged_blocks(prior_window[0], rows), length), "tm")
        cond = edged_blocks(conductivity, rows)[step_index]
        parts = tuple(
            x[:, at]
            for x in (got, jnp.stack([prior, cond]))
            for at in (slice(EDGE, -EDGE), slice(0, EDGE), slice(-EDGE, None))
        )

    table = sweep_table(length)
    table = jnp.broadcast_to(jnp.asarray(table)[..., None], table.shape + (LANES,))
    deep = rows + 2 * EDGE
    flat = pltpu.VMEM((length * deep, LANES), jnp.float32)
    stack = pltpu.VMEM((length, deep, LANES), jnp.float32)
    plane = pltpu.VMEM((deep, LANES), jnp.float32)
    correction = pl.pallas_call(
        functools.partial(solve_kernel, length, (height * halves, columns)),
        name="solve",
        out_shape=shape(length, rows // 2, LANES),
        in_specs=[SMEM] + [VMEM] * 7,
        out_specs=VMEM,
        scratch_shapes=[stack, stack, flat, flat, pltpu.VMEM((length * rows, LANES), jnp.float32)] + [plane] * 6,
        compiler_params=pltpu.CompilerParams(vmem_limit_bytes=VMEM_LIMIT if by_swaps else 2 * VMEM_LIMIT),
    )(place, *parts, table)

    back = lax.all_to_all(correction, "tm", split_axis=0, concat_axis=0, tiled=True)
    keep = rows // 2
    chunk = min(keep, 16)
    view = (bands, 2, keep, columns)
    updated = pl.pallas_call(
        merge_kernel,
        name="merge",
        grid=(keep // chunk,),
        out_shape=shape(*view),
        in_specs=[
            SMEM,
            pl.BlockSpec((bands, 2, chunk, columns), lambda i: (0, 0, i, 0)),
            pl.BlockSpec((across, bands, chunk, LANES), lambda i: (0, 0, i, 0)),
        ],
        out_specs=pl.BlockSpec((bands, 2, chunk, columns), lambda i: (0, 0, i, 0)),
        compiler_params=params,
    )(place, state.reshape(view), back.reshape(across, bands, keep, LANES))
    return updated.reshape(1, height, columns)


def solution(mesh):
    in_specs = (P("tm", "space", None), P("tm", "space", None), P("space", None))
    out_specs = P("tm", "space", None)
    return jax.shard_map(body, mesh=mesh, in_specs=in_specs, out_specs=out_specs, check_vma=False)
```

```python
import functools
import math

import jax
import jax.numpy as jnp
import numpy as np
from jax import lax
from jax.experimental import pallas as pl
from jax.experimental.pallas import tpu as pltpu
from jax.sharding import PartitionSpec as P

SWEEPS = 24
LANES = 128
WIDTH = LANES // 2
EDGE = 32
AHEAD = 6
PARTS = 4
EARLY = 11
INNER = 8

time_ratio = 2.0
window_alpha = 0.01
spectral_bound = 24.0

HALO_AHEAD = 6
PARTS = 4
EARLY = 11
INNER = 8
CENTER_STEP = 16
VMEM = pl.BlockSpec(memory_space=pltpu.VMEM)
VMEM_LIMIT = 20 * 1024 * 1024
SMEM = pl.BlockSpec(memory_space=pltpu.SMEM)
HBM = pl.BlockSpec(memory_space=pltpu.HBM)


def sweep_table(length):
    beta = math.exp(math.log(window_alpha) / length)
    half = 0.5 * spectral_bound * time_ratio

    def times_y(p):
        out = np.zeros_like(p)
        out[1:] += 0.5 * p[:-1]
        out[:-1] += 0.5 * p[1:]
        out[1] += 0.5 * p[0]
        return out

    def series(j):
        angle = 2.0 * math.pi * j / length
        shift = complex(1.0 - beta * math.cos(angle), beta * math.sin(angle))
        if j == 0 or 2 * j == length:
            shift = complex(shift.real, 0.0)
        center = shift + half
        rel = center / half
        x = np.zeros(SWEEPS + 3, np.complex128)
        r = x.copy()
        r[0] = 1.0
        d = r / center
        rho = 1.0 / rel
        for _ in range(SWEEPS):
            image = center * d - half * times_y(d)
            x = x + d
            r = r - image
            rho2 = 1.0 / (2.0 * rel - rho)
            d = rho2 * rho * d + (2.0 * rho2 / half) * r
            rho = rho2
        x = x + d
        second = 0.5 * x
        second[0] = x[0]
        second[:-2] -= 0.5 * x[2:]
        return second[: SWEEPS + 1]

    pairs = length // 2
    table = np.zeros((pairs, SWEEPS + 1, 4))
    for p in range(pairs):
        g = series(p)
        if p == 0:
            last = series(pairs)
            table[p] = np.stack([g.real, 0 * g.real, 0 * g.real, last.real], axis=1)
        else:
            table[p] = np.stack([g.real, -g.imag, g.imag, g.real], axis=1)
    return table.reshape(pairs // 8, 8, SWEEPS + 1, 4).transpose(0, 2, 3, 1).astype(np.float32)


def turned(value, angle):
    re, im = value
    c, s = math.cos(angle), math.sin(angle)
    if abs(s) < 1e-12:
        return (re * c if c != 1.0 else re), (None if im is None else im * c if c != 1.0 else im)
    if abs(c) < 1e-12:
        return (None if im is None else -im * s if s != -1.0 else im), (re * s if s != -1.0 else -re)
    if im is None:
        return re * c, re * s
    return re * c - im * s, re * s + im * c


def plus(a, b):
    return b if a is None else a if b is None else a + b


def minus(a, b):
    return a if b is None else -b if a is None else a - b


def negative(a):
    return None if a is None else -a


def real_dft(fields):
    count = len(fields)
    if count == 1:
        return [(fields[0], None)]
    even, odd = real_dft(fields[0::2]), real_dft(fields[1::2])
    out = [None] * (count // 2 + 1)
    for j in range(count // 4 + 1):
        if count == 2:
            e, o = even[0], odd[0]
        else:
            e, o = even[j], odd[j]
        t = turned(o, -2.0 * math.pi * j / count)
        mirror = (minus(e[0], t[0]), negative(minus(e[1], t[1])))
        out[count // 2 - j] = mirror
        out[j] = (plus(e[0], t[0]), plus(e[1], t[1]))
    out[0] = (out[0][0], None)
    out[-1] = (out[-1][0], None)
    return out


def real_inverse(spectrum):
    count = 2 * (len(spectrum) - 1)
    if count == 2:
        a, b = spectrum[0][0], spectrum[1][0]
        return [a + b, a - b]
    even, odd = [], []
    for j in range(count // 4 + 1):
        a, b = spectrum[j], spectrum[count // 2 - j]
        even.append((plus(a[0], b[0]), minus(a[1], b[1])))
        t = (minus(a[0], b[0]), plus(a[1], b[1]))
        odd.append(turned_full(t, 2.0 * math.pi * j / count))
    even[0] = (even[0][0], None)
    even[-1] = (even[-1][0], None)
    odd[0] = (odd[0][0], None)
    odd[-1] = (odd[-1][0], None)
    even, odd = real_inverse(even), real_inverse(odd)
    return [v for pair in zip(even, odd) for v in pair]


def turned_full(value, angle):
    re, im = value
    if re is None:
        c, s = math.cos(angle), math.sin(angle)
        return (-im * s if abs(s) > 1e-12 else None), (im * c if abs(c) > 1e-12 else None)
    return turned(value, angle)


def conductance(conductivity, values):
    return conductivity * (1.0 + 0.5 * jnp.tanh(values))


def roll(x, amount):
    return pltpu.roll(x, amount % LANES, x.ndim - 1)


def lane_index():
    return lax.broadcasted_iota(jnp.int32, (8, LANES), 1)


def patch(tiles, lane, cb):
    zero = jnp.zeros((8, LANES), jnp.float32)
    tile = lambda c: tiles[c] if 0 <= c < len(tiles) else zero
    if cb % 2 == 0:
        return roll(jnp.where(lane < LANES - EDGE, tile(cb // 2), tile(cb // 2 - 1)), EDGE)
    return roll(jnp.where(lane < EDGE, tile(cb // 2 + 1), tile(cb // 2)), -EDGE)


def pack_kernel(place_ref, field_ref, out_ref, given, made, arrive, leave):
    bands, height, columns = field_ref.shape
    ranks = out_ref.shape[0]
    flip = place_ref[0]
    lane = lane_index()
    chunk = height // PARTS
    parts = [pl.ds(i * chunk, chunk) for i in range(PARTS)]
    loads = [pltpu.make_async_copy(field_ref.at[:, p], given.at[:, p], arrive.at[i]) for i, p in enumerate(parts)]
    stores = [
        pltpu.make_async_copy(made.at[:, :, :, p], out_ref.at[:, :, :, p], leave.at[i]) for i, p in enumerate(parts)
    ]
    for load in loads:
        load.start()
    for i in range(PARTS):
        loads[i].wait()
        for t in range(i * chunk // 8, (i + 1) * chunk // 8):
            at = pl.ds(t * 8, 8)
            for band in range(bands):
                tiles = [given[band, at, pl.ds(c * LANES, LANES)] for c in range(columns // LANES)]
                for cb in range(columns // WIDTH):
                    made[cb % ranks, cb // ranks, lax.bitwise_xor(band, flip), at, :] = patch(tiles, lane, cb)
        stores[i].start()
    for store in stores:
        store.wait()


def share_kernel(place_ref, field_ref, out_ref):
    bands, height, columns = field_ref.shape
    flip = place_ref[0]
    lane = lane_index()
    ranks = columns // WIDTH // 2
    for band in range(bands):
        for side in range(2):
            to = side * bands + lax.bitwise_xor(band, flip)

            def tile(c, t):
                tiles = [field_ref[band, pl.ds(t, 8), pl.ds(i * LANES, LANES)] for i in range(columns // LANES)]
                return patch(tiles, lane, side * ranks + 2 * c)

            for c in range(ranks // 2):
                for t in range(0, height, 8):
                    out_ref[to, pl.ds(c * height + t, 8), :] = tile(c, t)
            for t in range(0, height // 2, 8):
                low, high = tile(ranks // 2, t), tile(ranks // 2, height // 2 + t)
                out_ref[to, pl.ds(ranks // 2 * height + t, 8), :] = jnp.where(lane < WIDTH, low, roll(high, WIDTH))


def cut_kernel(place_ref, *refs):
    *quarters, out_ref = refs
    ranks, height, _ = out_ref.shape
    lane = lane_index()
    mine = place_ref[9]

    def tile(at):
        value = quarters[-1][at, :]
        for i, ref in enumerate(quarters[:-1]):
            value = jnp.where(mine == i, ref[at, :], value)
        return value

    for t in range(0, height, 8):
        tiles = [tile(pl.ds(c * height + t, 8)) for c in range(ranks // 2)]
        folded = tile(pl.ds(ranks // 2 * height + t % (height // 2), 8))
        tiles.append(folded if t < height // 2 else roll(folded, WIDTH))
        for z in range(ranks):
            value = tiles[z // 2] if z % 2 == 0 else roll(jnp.where(lane < WIDTH, tiles[z // 2 + 1], tiles[z // 2]), WIDTH)
            out_ref[z, pl.ds(t, 8), :] = value


def own_kernel(place_ref, field_ref, out_ref):
    height, columns = field_ref.shape[1:]
    band, block = place_ref[1], place_ref[2]
    lane = lane_index()
    for cb in range(columns // WIDTH):
        @pl.when(block == cb)
        def _():
            for t in range(height // 8):
                at = pl.ds(t * 8, 8)
                tiles = [field_ref[band, at, pl.ds(c * LANES, LANES)] for c in range(columns // LANES)]
                out_ref[at, :] = patch(tiles, lane, cb)


def residual_tile(length, start, limits, place_ref, state, coeff, prior, lane, store):
    beta = math.exp(math.log(window_alpha) / length)
    here, above, below = pl.ds(start, 8), pl.ds(start - 1, 8), pl.ds(start + 1, 8)
    inside = inside_rows(start, limits, place_ref, lane)
    fields = []
    for n in range(length):
        v, vn, vs = state[n, here, :], state[n, above, :], state[n, below, :]
        c, cn, cs = coeff[n, here, :], coeff[n, above, :], coeff[n, below, :]
        fe = (c + roll(c, -1)) * (roll(v, -1) - v)
        fs = (c + cs) * (vs - v)
        fn = (c + cn) * (vn - v)
        flux = (0.5 * time_ratio) * (fe - roll(fe, 1) + fs + fn)
        before = prior[here, :] if n == 0 else state[n - 1, here, :]
        r = jnp.where(inside, before - v + flux, 0.0)
        fields.append(r * (beta**n))
    spectrum = real_dft(fields)
    pairs = length // 2
    for p in range(pairs):
        store(p, spectrum[p][0], spectrum[pairs][0] if p == 0 else spectrum[p][1])


def inside_rows(start, limits, place_ref, lane):
    sub = lax.broadcasted_iota(jnp.int32, (8, LANES), 0)
    row, column = sub + (place_ref[3] + start), lane + place_ref[4]
    return (row >= 0) & (row < limits[0]) & (column >= 0) & (column < limits[1])


def put_weights(start, limits, place_ref, lane, frozen, weights, scale):
    south, east, west, middle = weights
    here, above, below = pl.ds(start, 8), pl.ds(start - 1, 8), pl.ds(start + 1, 8)
    inside = inside_rows(start, limits, place_ref, lane)
    q, qn, qs = frozen[here, :], frozen[above, :], frozen[below, :]
    qe, qw = roll(q, -1), roll(q, 1)
    middle[here, :] = 2.0 - scale * (4.0 * q + qn + qs + qe + qw)
    south[here, :] = jnp.where(inside & inside_rows(start + 1, limits, place_ref, lane), scale * (q + qs), 0.0)
    ew = jnp.where(inside & (lane + place_ref[4] + 1 < limits[1]), scale * (q + qe), 0.0)
    east[here, :] = ew
    west[here, :] = roll(ew, 1)


def weight_scale():
    return 0.5 * time_ratio * 2.0 / (0.5 * spectral_bound * time_ratio)


def pair_at(ref, base, i):
    at = base + i * 16
    return ref[pl.ds(at, 8), :], ref[pl.ds(at + 8, 8), :]


def sweep(begin, end, weights, cur, old, new, base):
    south, east, west, middle = weights

    def weight(ref, i):
        return ref[pl.ds(i, 8, stride=0), :]

    def across(i, here):
        we, ww = weight(east, i), weight(west, i)
        return tuple(we * roll(x, -1) + ww * roll(x, 1) for x in here)

    ahead = min(AHEAD, end - begin)
    values = {i: cur(i) for i in range(begin - 1, begin + ahead)}
    flows = {i: across(i, values[i]) for i in range(begin, begin + ahead)}
    wn = weight(south, begin - 1)
    for i in range(begin, end):
        j = i + ahead
        if j <= end:
            values[j] = cur(j)
        if j < end:
            flows[j] = across(j, values[j])
        ws, wc = weight(south, i), weight(middle, i)
        flow = flows.pop(i)
        above, here, below = values.pop(i - 1), values[i], values[i + 1]
        last = old and old(i)
        for x in range(2):
            value = wc * here[x] + wn * above[x] + ws * below[x]
            value = value + flow[x]
            if last:
                value = value - last[x]
            new[pl.ds(base + i * 16 + 8 * x, 8), :] = value
        wn = ws


def gain(row, terms, values, start):
    parts = list(start) if start else [None, None]
    for h, (a, b) in zip(terms, values):
        for x in range(2):
            parts[x] = plus(parts[x], h[2 * x] * a + h[2 * x + 1] * b)
    return parts


def early_sweeps(rows):
    return EARLY if rows - 2 * INNER > 2 * EARLY + 8 else 0


def begin_kernel(
    length, limits, place_ref, w_ref, own_ref, table_ref, even_ref, odd_ref, sum_ref,
    coeff, frozen, south, east, west, middle,
):
    rows = w_ref.shape[1]
    lane = lane_index()
    count = rows - 2 * INNER
    wide = 2 if count % 16 == 0 else 1
    weights = south, east, west, middle

    def coefficients(t, _):
        for u in range(2):
            at = pl.ds(pl.multiple_of(t * 16, 16) + u * 8, 8)
            cond = own_ref[1, at, :]
            frozen[at, :] = conductance(cond, own_ref[0, at, :])
            for n in range(length):
                coeff[n, at, :] = conductance(cond, w_ref[n, at, :])
        return 0

    lax.fori_loop(0, rows // 16, coefficients, 0)

    def residuals(t, _):
        for u in range(wide):
            at = (t * wide + u) * 8

            def store(p, re, im):
                base = ((p // 8) * count + at) * 16 + p % 8
                even_ref[pl.ds(base, 8, stride=16), :] = re
                even_ref[pl.ds(base + 8, 8, stride=16), :] = im

            residual_tile(length, INNER + at, limits, place_ref, w_ref, coeff, own_ref.at[0], lane, store)
        return 0

    lax.fori_loop(0, count // (8 * wide), residuals, 0)
    levels = early_sweeps(rows)
    if levels == 0:
        return
    for start in range(INNER, rows - INNER, 8):
        put_weights(start, limits, place_ref, lane, frozen, weights, weight_scale())

    def sweeps(g, _):
        base = (g * count - INNER) * 16
        refs = even_ref, odd_ref
        for level in range(1, levels + 1):
            begin, end = INNER + level, rows - INNER - level
            cur, new = refs[(level - 1) % 2], refs[level % 2]
            old = functools.partial(pair_at, new, base) if level > 1 else None
            sweep(begin, end, weights, functools.partial(pair_at, cur, base), old, new, base)
            if level % 2 == 1:
                terms = [[table_ref[g, k, i] for i in range(4)] for k in (level - 1, level)]
                for i in range(begin, end):
                    start = pair_at(sum_ref, base, i) if level > 1 else None
                    parts = gain(i, terms, [pair_at(cur, base, i), pair_at(new, base, i)], start)
                    for x in range(2):
                        sum_ref[pl.ds(base + i * 16 + 8 * x, 8), :] = parts[x]
        return 0

    groups = length // 16
    if groups == 1:
        sweeps(0, 0)
    else:
        lax.fori_loop(0, groups, sweeps, 0)


def solve_kernel(
    length, limits, place_ref, w_ref, wa_ref, wb_ref, own_ref, owna_ref, ownb_ref, even_ref, odd_ref, sum_ref, table_ref,
    out_ref,
    state, coeff, field, other, total, prior, frozen, south, east, west, middle,
):
    rows = w_ref.shape[1]
    deep = state.shape[1]
    pairs = length // 2
    groups = pairs // 8
    low = EDGE - SWEEPS
    lane = lane_index()
    beta = math.exp(math.log(window_alpha) / length)
    weights = south, east, west, middle
    first_inner, last_inner = EDGE + INNER, EDGE + rows - INNER

    def edge_pair(first, second):
        def read(a, b, n, at):
            return jnp.where(first == 1, a[n, at, :], jnp.where(second == 1, b[n, at, :], 0.0))
        return read

    upper, lower = edge_pair(place_ref[5], place_ref[6]), edge_pair(place_ref[7], place_ref[8])
    spare = min(2 * INNER, rows // 2)

    def gather(begin, end):
        for to in range(begin, end, 8):
            where = pl.ds(to, 8)
            for i in (0, 1):
                if to < EDGE:
                    value = upper(owna_ref, ownb_ref, i, where)
                elif to < EDGE + rows:
                    value = own_ref[i, pl.ds(to - EDGE, 8), :]
                else:
                    value = lower(owna_ref, ownb_ref, i, pl.ds(to - EDGE - rows, 8))
                if i == 0:
                    prior[where, :] = value
                    p = value
                else:
                    cond = value
            frozen[where, :] = conductance(cond, p)
            if EDGE + spare <= to < EDGE + rows - spare:
                continue
            for n in range(length):
                if to < EDGE:
                    v = upper(wa_ref, wb_ref, n, where)
                elif to < EDGE + rows:
                    v = w_ref[n, pl.ds(to - EDGE, 8), :]
                else:
                    v = lower(wa_ref, wb_ref, n, pl.ds(to - EDGE - rows, 8))
                state[n, where, :] = v
                coeff[n, where, :] = conductance(cond, v)

    gather(0, deep)

    south[pl.ds(0, 8), :] = jnp.zeros((8, LANES), jnp.float32)
    for start in range(low, deep - low, 8):
        put_weights(start, limits, place_ref, lane, frozen, weights, weight_scale())

    ends = [(low, first_inner), (last_inner, deep - low)]
    for begin, end in ends:
        def residuals(t, _):
            for u in range(2):
                start = begin + t * 16 + u * 8

                def store(p, re, im):
                    base = ((p // 8) * deep + start) * 16 + p % 8
                    field[pl.ds(base, 8, stride=16), :] = re
                    field[pl.ds(base + 8, 8, stride=16), :] = im

                residual_tile(length, start, limits, place_ref, state, coeff, prior, lane, store)
            return 0

        lax.fori_loop(0, (end - begin) // 16, residuals, 0)

    levels = early_sweeps(rows)

    def sweeps(g, _):
        base = g * (deep * 16)
        total_base = (g * rows - EDGE) * 16
        inner_base = (g * (rows - 2 * INNER) - first_inner) * 16
        inner, refs = (even_ref, odd_ref), (field, other)

        def early(level, i):
            return level <= levels and first_inner + level <= i < last_inner - level

        def read(level, i):
            if early(level, i):
                return pair_at(inner[level % 2], inner_base, i)
            return pair_at(refs[level % 2], base, i)

        begun = set()

        def accumulate(pair):
            terms = [[table_ref[g, k, i] for i in range(4)] for k in pair]
            for i in range(EDGE, EDGE + rows):
                if early(pair[-1], i):
                    continue
                if i in begun:
                    start = pair_at(total, total_base, i)
                else:
                    start = pair_at(sum_ref, inner_base, i) if levels and early(1, i) else None
                begun.add(i)
                parts = gain(i, terms, [read(k, i) for k in pair], start)
                for x in range(2):
                    total[pl.ds(total_base + i * 16 + 8 * x, 8), :] = parts[x]

        for level in range(1, SWEEPS + 1):
            begin, end = low + level, deep - low - level
            ranges = [(begin, end)]
            if level <= levels:
                ranges = [(begin, first_inner + level), (last_inner - level, end)]
            cur = functools.partial(read, level - 1)
            old = functools.partial(read, level - 2) if level > 1 else None
            for some in ranges:
                sweep(*some, weights, cur, old, refs[level % 2], base)
            if level % 2 == 1:
                accumulate((level - 1, level))
        if SWEEPS % 2 == 0:
            accumulate((SWEEPS,))
        return 0

    if groups == 1:
        sweeps(0, 0)
    else:
        lax.fori_loop(0, groups, sweeps, 0)

    keep = rows // 2

    def inverse(start):
        spectrum = []
        nyquist = None
        for p in range(pairs):
            base = (p // 8) * rows * 16 + start * 16 + p % 8
            re = total[pl.ds(base, 8, stride=16), :]
            im = total[pl.ds(base + 8, 8, stride=16), :]
            if p == 0:
                nyquist = im
                im = None
            spectrum.append((re, im))
        spectrum.append((nyquist, None))
        return real_inverse(spectrum)

    def finish(t, _):
        for u in range(wide):
            finish_tile(t * wide + u)
        return 0

    wide = 2 if keep % 16 == 0 else 1

    def finish_tile(t):
        lower, upper = inverse(t * 8), inverse(keep + t * 8)
        for n in range(length):
            factor = beta ** (-n) / length
            merged = jnp.where(lane < WIDTH, roll(lower[n], -EDGE), roll(upper[n], EDGE))
            out_ref[n, pl.ds(pl.multiple_of(t * 8, 8), 8), :] = merged * factor

    lax.fori_loop(0, keep // (8 * wide), finish, 0)


def merge_kernel(place_ref, w_ref, got_ref, out_ref, made, leave):
    bands, _, height, columns = w_ref.shape
    ranks = got_ref.shape[0]
    flip = place_ref[0]
    lane = lane_index()
    chunk = height // PARTS if height % (8 * PARTS) == 0 else height
    parts = [pl.ds(i * chunk, chunk) for i in range(height // chunk)]
    stores = [
        pltpu.make_async_copy(made.at[:, :, p], out_ref.at[:, :, p], leave.at[i]) for i, p in enumerate(parts)
    ]
    for i, store in enumerate(stores):
        for t in range(i * chunk // 8, (i + 1) * chunk // 8):
            at = pl.ds(t * 8, 8)
            for band in range(bands):
                for pair in range(columns // LANES):
                    a, b = (
                        got_ref[cb % ranks, cb // ranks, lax.bitwise_xor(band, flip), at, :]
                        for cb in (2 * pair, 2 * pair + 1)
                    )
                    cols = pl.ds(pair * LANES, LANES)
                    made[band, 0, at, cols] = w_ref[band, 0, at, cols] + jnp.where(lane < WIDTH, a, roll(b, WIDTH))
                    made[band, 1, at, cols] = w_ref[band, 1, at, cols] + jnp.where(lane < WIDTH, roll(a, WIDTH), b)
        store.start()
    for store in stores:
        store.wait()


def spread(parts, axis, stride):
    owner = lax.axis_size(axis) - 1
    base = [owner - (stride - 1) + low for low in range(stride)]
    radix = len(parts)
    routes = [[(b, b - stride * (radix - 1 - v)) for b in base] for v in range(radix - 1)]
    return [lax.ppermute(part, axis, route) for part, route in zip(parts, routes)] + [parts[-1]]


def scattered(blocks, axis, stride=1):
    count = lax.axis_size(axis)
    index = lax.axis_index(axis)
    current = blocks
    while True:
        radix = current.shape[0]
        digit = (index // stride) % radix
        *others, kept = spread(list(current), axis, stride)
        for value, other in enumerate(others):
            kept = jnp.where(digit == value, other, kept)
        stride *= radix
        if stride == count:
            return kept[0]
        current = by_digit(kept, count // stride)


def first_radix(count):
    return 4 if count % 4 == 0 else 2


def by_digit(blocks, count):
    radix = first_radix(count)
    return blocks.reshape((count // radix, radix) + blocks.shape[1:]).swapaxes(0, 1)


def swapped(values, axis, distance=1):
    count = lax.axis_size(axis)
    return lax.ppermute(values, axis, [(i, i ^ distance) for i in range(count)])


def edged_blocks(field, rows):
    halves = lax.axis_size("space")
    up = lax.ppermute(field[:EDGE], "space", [(i + 1, i) for i in range(halves - 1)])
    down = lax.ppermute(field[-EDGE:], "space", [(i, i + 1) for i in range(halves - 1)])
    field = jnp.pad(jnp.concatenate([down, field, up]), ((0, 0), (EDGE, EDGE)))
    height, columns = field.shape
    return jnp.stack(
        [
            field[r : r + rows + 2 * EDGE, c : c + LANES]
            for c in range(0, columns - 2 * EDGE, WIDTH)
            for r in range(0, height - 2 * EDGE, rows)
        ]
    )


def body(window_state, prior_window, conductivity):
    length = lax.axis_size("tm")
    halves = lax.axis_size("space")
    height, columns = window_state.shape[1:]
    across = columns // WIDTH
    rows = height * across // length
    bands = height // rows
    step_index = lax.axis_index("tm")
    half_index = lax.axis_index("space")
    state = window_state[0]
    by_swaps = halves == 2 and bands == 2 and rows >= EDGE and across % 4 == 0
    flip = half_index if by_swaps else 0
    ranks = across // 2 if by_swaps else across
    band = (step_index % bands) ^ flip
    block = step_index // bands % (across // ranks) * ranks + step_index // (length // ranks)
    overall = half_index * bands + band
    odd = overall % 2
    if by_swaps:
        sides = [odd, (overall == 2), 1 - odd, (overall == 1)]
    else:
        sides = [1, 0, 0, 1]
    place = jnp.stack(
        [
            jnp.asarray(v, jnp.int32)
            for v in [flip, band, block, overall * rows - EDGE, block * WIDTH - EDGE] + sides + [step_index % 4]
        ]
    )

    begin_place = place.at[3].add(EDGE)

    shape = lambda *dims: jax.ShapeDtypeStruct(dims, jnp.float32)
    params = pltpu.CompilerParams(vmem_limit_bytes=VMEM_LIMIT)

    def packed(field):
        return pl.pallas_call(
            pack_kernel,
            name="pack",
            out_shape=shape(ranks, across // ranks, bands, rows, LANES),
            in_specs=[SMEM, HBM],
            out_specs=HBM,
            scratch_shapes=[
                pltpu.VMEM((bands, rows, columns), jnp.float32),
                pltpu.VMEM((ranks, across // ranks, bands, rows, LANES), jnp.float32),
                pltpu.SemaphoreType.DMA((PARTS,)),
                pltpu.SemaphoreType.DMA((PARTS,)),
            ],
            compiler_params=params,
        )(place, pltpu.with_memory_space_constraint(field.reshape(bands, rows, columns), pltpu.HBM)).reshape(length, rows, LANES)

    if by_swaps:
        sent = packed(state)
        got = lax.all_to_all(sent, "tm", split_axis=0, concat_axis=0, tiled=True)
        quarters = pl.pallas_call(
            share_kernel,
            name="share",
            out_shape=shape(4, (ranks + 1) * rows // 2, LANES),
            in_specs=[SMEM, VMEM],
            out_specs=VMEM,
            compiler_params=params,
        )(place, prior_window[0].reshape(bands, rows, columns))
        mine = pl.pallas_call(
            cut_kernel,
            name="cut",
            out_shape=shape(ranks, rows, LANES),
            in_specs=[SMEM] + [VMEM] * 4,
            out_specs=VMEM,
            compiler_params=params,
        )(place, *spread(list(quarters), "tm", 1))
        prior = scattered(by_digit(mine, ranks), "tm", 4)
        cond = pl.pallas_call(
            own_kernel,
            name="own",
            out_shape=shape(rows, LANES),
            in_specs=[SMEM, VMEM],
            out_specs=VMEM,
            compiler_params=params,
        )(place, conductivity.reshape(bands, rows, columns))
        own = jnp.stack([prior, cond])

        def edges(blocks):
            beside = swapped(jnp.where(odd == 1, blocks[:, :EDGE], blocks[:, -EDGE:]), "tm")
            across_half = swapped(jnp.where(half_index == 1, blocks[:, :EDGE], blocks[:, -EDGE:]), "space")
            return beside, across_half

        parts = (got,) + edges(got) + (own,) + edges(own)
    else:
        got = lax.all_to_all(edged_blocks(state, rows), "tm", split_axis=0, concat_axis=0, tiled=True)
        prior = scattered(by_digit(edged_blocks(prior_window[0], rows), length), "tm")
        cond = edged_blocks(conductivity, rows)[step_index]
        parts = tuple(
            x[:, at]
            for x in (got, jnp.stack([prior, cond]))
            for at in (slice(EDGE, -EDGE), slice(0, EDGE), slice(-EDGE, None))
        )

    table = sweep_table(length)
    table = jnp.broadcast_to(jnp.asarray(table)[..., None], table.shape + (LANES,))
    deep = rows + 2 * EDGE
    flat = pltpu.VMEM((length * deep, LANES), jnp.float32)
    stack = pltpu.VMEM((length, deep, LANES), jnp.float32)
    plane = pltpu.VMEM((deep, LANES), jnp.float32)
    inner = pl.pallas_call(
        functools.partial(begin_kernel, length, (height * halves, columns)),
        name="begin",
        out_shape=[shape(length * max(rows - 2 * INNER, 8), LANES)] * 3,
        in_specs=[SMEM, VMEM, VMEM, VMEM],
        out_specs=[VMEM] * 3,
        scratch_shapes=[pltpu.VMEM((length, rows, LANES), jnp.float32)] + [pltpu.VMEM((rows, LANES), jnp.float32)] * 5,
        compiler_params=params,
    )(begin_place, parts[0], parts[3], table)
    correction = pl.pallas_call(
        functools.partial(solve_kernel, length, (height * halves, columns)),
        name="solve",
        out_shape=shape(length, rows // 2, LANES),
        in_specs=[SMEM] + [VMEM] * 10,
        out_specs=VMEM,
        scratch_shapes=[stack, stack, flat, flat, pltpu.VMEM((length * rows, LANES), jnp.float32)] + [plane] * 6,
        compiler_params=pltpu.CompilerParams(vmem_limit_bytes=VMEM_LIMIT if by_swaps else 2 * VMEM_LIMIT),
    )(place, *parts, *inner, table)

    back = lax.all_to_all(correction, "tm", split_axis=0, concat_axis=0, tiled=True)
    keep = rows // 2
    view = (bands, 2, keep, columns)
    updated = pl.pallas_call(
        merge_kernel,
        name="merge",
        out_shape=shape(*view),
        in_specs=[SMEM, VMEM, VMEM],
        out_specs=HBM,
        scratch_shapes=[pltpu.VMEM(view, jnp.float32), pltpu.SemaphoreType.DMA((PARTS,))],
        compiler_params=params,
    )(place, state.reshape(view), back.reshape(ranks, across // ranks, bands, keep, LANES))
    return updated.reshape(1, height, columns)


def solution(mesh):
    in_specs = (P("tm", "space", None), P("tm", "space", None), P("space", None))
    out_specs = P("tm", "space", None)
    return jax.shard_map(body, mesh=mesh, in_specs=in_specs, out_specs=out_specs, check_vma=False)
```
